32 devices in a mesh: dp: 8 (over z, core), mp: 4 (over y, x).
Axes of the slice: x: 2, y: 2, z: 4, core: 2. Of those that a mesh axis runs over, the one named last changes fastest.
Arguments:
- activations: bfloat16 [4096, 8192], P('dp', 'mp')
- value_grad: bfloat16 [4096, 1024], P('dp'), may hold values from -6 to 6
- master: float32 [8192, 1024], P(('mp', 'dp')), may hold values from -6 to 6
- first_moment: float32 [8192, 1024], P(('mp', 'dp')), may hold values from -2 to 2
- second_moment: float32 [8192, 1024], P(('mp', 'dp')), may hold values from 0.05 to 1
- step_count: int32 [1], replicated, may hold values from 1 to 40
Outputs:
- new_master: float32 [8192, 1024], P(('mp', 'dp'))
- new_first: float32 [8192, 1024], P(('mp', 'dp'))
- new_second: float32 [8192, 1024], P(('mp', 'dp'))
- rollout_update: bfloat16 [8192, 1024], P(None, 'mp')
The draws below stay inside these ranges and needn't reach their ends.
Inputs may be any that keep to these rules, and one draw needn't show every extreme that they name: `step_count`: the number of optimizer steps taken so far, this one included.
All inputs are finite; a program needn't handle non-finite values.
Results may differ from the reference program's by a relative error of at most 0.0004.
Values may be sent and summed in bfloat16 or wider, within the bound.
A program may use at most 64 MiB of HBM per device.

```python
import math
import jax
import jax.numpy as jnp
from jax import lax

D = 8192
KV = 1024
TOKENS = 4096


def draw_activations(key, part):
    key_base, key_spread = jax.random.split(key, 2)
    values_drawn = jax.random.normal(key_base, (TOKENS, D), jnp.float32)
    column_ramp = jnp.exp(jnp.log(3.0) * jnp.arange(D, dtype=jnp.float32) / D)
    column_spread = 10.0 ** jax.random.uniform(key_spread, (D,), jnp.float32) / 3.0
    values_drawn = jnp.clip(values_drawn * column_ramp * column_spread, -40.0, 40.0)
    return values_drawn.astype(jnp.bfloat16)


def block_scale(stream_key, dims, pieces, smallest, high):
    level, own = 1.0, jax.random.fold_in(stream_key, 6)
    for axis_at, blocks in pieces:
        draws = jnp.exp(jax.random.uniform(jax.random.fold_in(own, axis_at), (blocks,), jnp.float32, smallest / len(pieces), high / len(pieces)))
        level = level * jnp.repeat(draws, dims[axis_at] // blocks).reshape([-1 if axis == axis_at else 1 for axis in range(len(dims))])
    return level


def normal_values(stream_key, dims, width, most, pieces=(), kind=jnp.bfloat16):
    result = width * jax.random.normal(stream_key, dims, jnp.float32)
    if pieces:
        result = result * block_scale(stream_key, dims, pieces, -0.22, 0.18)
    return jnp.clip(result, -most, most).astype(kind)


def setup_inputs(seed: int = 0) -> dict:
    arg_keys = jax.random.split(jax.random.key(seed), 7)
    activations = draw_activations(jax.random.fold_in(arg_keys[6], 71), 0)
    value_grad = normal_values(arg_keys[1], (TOKENS, KV), 1.0, 6.0, ((0, 8),))
    master = normal_values(arg_keys[2], (D, KV), 1.0, 6.0, ((0, 32),), jnp.float32)
    first_moment = normal_values(arg_keys[3], (D, KV), 0.3, 2.0, ((0, 32),), jnp.float32)
    second_moment = jnp.clip(jnp.exp(math.log(1.0) - 2.9957323 * jax.random.uniform(arg_keys[4], (D, KV), jnp.float32) ** block_scale(arg_keys[4], (D, KV), ((0, 32),), -0.2, 0.2)), 0.05, 1.0)
    step_count = jax.random.randint(arg_keys[5], (1,), 1, 41).astype(jnp.int32)
    return {"activations": activations, "value_grad": value_grad, "master": master, "first_moment": first_moment, "second_moment": second_moment, "step_count": step_count}


def reference(activations, value_grad, master, first_moment, second_moment, step_count):
    grad = lax.dot_general(activations, value_grad, (((0,), (0,)), ((), ())), preferred_element_type=jnp.float32)
    norm_value = jnp.sqrt(jnp.sum(grad * grad))
    clip_total = 0.5 * jnp.sqrt(jnp.float32(D * KV))
    factor = jnp.minimum(jnp.float32(1.0), clip_total / (norm_value + 1e-06))
    clipped = factor * grad
    new_first = 0.9 * first_moment + 0.1 * clipped
    new_second = 0.95 * second_moment + 0.05 * clipped * clipped
    steps_done = step_count[0].astype(jnp.float32)
    bias_first = 1.0 - jnp.exp(steps_done * jnp.log(jnp.float32(0.9)))
    bias_second = 1.0 - jnp.exp(steps_done * jnp.log(jnp.float32(0.95)))
    direction = new_first / bias_first / (jnp.sqrt(new_second / bias_second) + 1e-08) + 0.1 * master
    new_master = master - 0.01 * direction
    return (new_master, new_first, new_second, direction.astype(jnp.bfloat16))
```

```python
import functools
import math

import jax
import jax.numpy as jnp
from jax import lax
from jax.experimental import pallas as pl
from jax.experimental.pallas import tpu as pltpu
from jax.sharding import PartitionSpec as P

F32 = jnp.float32
LEVELS = 32760.0
MESH = pl.DeviceIdType.MESH


def adam_terms(step):
    bias_first = 1.0 - jnp.exp(step * jnp.float32(math.log(0.9)))
    bias_second = 1.0 - jnp.exp(step * jnp.float32(math.log(0.95)))
    return 1.0 / bias_first, 1.0 / bias_second


def kernel(
    line,
    heads,
    chunks,
    clip_total,
    step_ref,
    act_ref,
    vg_ref,
    master_ref,
    first_ref,
    second_ref,
    new_master_ref,
    new_first_ref,
    new_second_ref,
    rollout_ref,
    act,
    vg,
    acc,
    q_out,
    s_out,
    q_in,
    s_in,
    norm_dp,
    norm_mp,
    w_in,
    m_in,
    v_in,
    w_out,
    m_out,
    v_out,
    update,
    in_sem,
    pair_send,
    pair_recv,
    load_sem,
    rs_send,
    rs_recv,
    norm_dp_send,
    norm_dp_recv,
    norm_mp_send,
    norm_mp_recv,
    store_sem,
    a2a_send,
    a2a_recv,
    up_send,
    down_send,
    chain_recv,
    mate_send,
    mate_recv,
):
    dpn = 2 * line
    dp = lax.axis_index("dp")
    mp = lax.axis_index("mp")
    z = dp // 2
    core = lax.rem(dp, 2)
    mate = dp + 1 - 2 * core
    tokens = act_ref.shape[0]
    rows = master_ref.shape[0]
    cols = master_ref.shape[1]
    part = rows // chunks
    head_cols = cols // heads
    tile = min(256, cols)

    barrier = pltpu.get_barrier_semaphore()
    for step in range(1, dpn):
        pl.semaphore_signal(
            barrier, inc=1, device_id={"dp": lax.rem(dp + step, dpn)}, device_id_type=MESH
        )
    for step in range(1, heads):
        pl.semaphore_signal(
            barrier, inc=1, device_id={"mp": lax.rem(mp + step, heads)}, device_id_type=MESH
        )

    lower = z < line // 2
    def owner(e):
        return jnp.where(lower, e, line - 1 - e)

    u = jnp.where(lower, z, line - 1 - z)

    def own_act(e):
        dest = owner(e)
        start = pl.multiple_of((dest * 2 + core) * rows, rows)
        return pltpu.make_async_copy(
            act_ref.at[:, pl.ds(start, rows)],
            act.at[dest, pl.ds(0, tokens)],
            in_sem.at[dest],
        )

    def own_vg():
        return pltpu.make_async_copy(vg_ref, vg.at[pl.ds(0, tokens)], in_sem.at[line])

    def pair_act(e):
        dest = owner(e)
        start = pl.multiple_of((dest * 2 + 1 - core) * rows, rows)
        return pltpu.make_async_remote_copy(
            src_ref=act_ref.at[:, pl.ds(start, rows)],
            dst_ref=act.at[dest, pl.ds(tokens, tokens)],
            send_sem=pair_send.at[dest],
            recv_sem=pair_recv.at[dest],
            device_id={"dp": mate},
            device_id_type=MESH,
        )

    def pair_vg():
        return pltpu.make_async_remote_copy(
            src_ref=vg_ref,
            dst_ref=vg.at[pl.ds(tokens, tokens)],
            send_sem=pair_send.at[line],
            recv_sem=pair_recv.at[line],
            device_id={"dp": mate},
            device_id_type=MESH,
        )

    order = list(range(line - 1, -1, -1))
    own_vg().start()
    for e in order:
        own_act(e).start()
    loads = [
        pltpu.make_async_copy(src, dst, load_sem.at[i])
        for i, (src, dst) in enumerate(
            ((master_ref, w_in), (first_ref, m_in), (second_ref, v_in))
        )
    ]
    pl.semaphore_wait(barrier, dpn - 1 + heads - 1)
    pair_act(order[0]).start()
    pair_vg().start()
    for e in order[1:]:
        pair_act(e).start()
    for copy in loads:
        copy.start()

    def multiply(e):
        dest = owner(e)
        own_act(e).wait()
        pair_act(e).wait_recv()

        @pl.loop(0, cols // tile)
        def _(n):
            at = pl.ds(pl.multiple_of(n * tile, tile), tile)
            acc[dest, :, at] = lax.dot_general(
                act[dest], vg[:, at], (((0,), (0,)), ((), ())), preferred_element_type=F32
            )

    def hop(dest, way, chunk):
        to = (z + 1 - 2 * way) * 2 + core
        data = pltpu.make_async_remote_copy(
            src_ref=q_out.at[dest, chunk],
            dst_ref=q_in.at[way, dest, chunk],
            send_sem=rs_send.at[0, dest, chunk],
            recv_sem=rs_recv.at[0, way, dest, chunk],
            device_id={"dp": to},
            device_id_type=MESH,
        )
        scale = pltpu.make_async_remote_copy(
            src_ref=s_out.at[dest, chunk],
            dst_ref=s_in.at[way, dest, chunk],
            send_sem=rs_send.at[1, dest, chunk],
            recv_sem=rs_recv.at[1, way, dest, chunk],
            device_id={"dp": to},
            device_id_type=MESH,
        )
        return data, scale

    def take(dest, way, chunk):
        for copy in hop(dest, way, chunk):
            copy.wait_recv()
        at = pl.ds(pl.multiple_of(chunk * part, part), part)
        for n in range(0, cols, tile):
            here = slice(n, n + tile)
            got = q_in[way, dest, chunk, :, here].astype(jnp.int32).astype(F32)
            acc[dest, at, here] += got * (s_in[way, dest, chunk, :, here] * (1.0 / LEVELS))

    def give(dest, way, chunk):
        at = pl.ds(pl.multiple_of(chunk * part, part), part)
        for n in range(0, cols, tile):
            here = slice(n, n + tile)
            total = acc[dest, at, here]
            top = jnp.maximum(jnp.max(jnp.abs(total), axis=0, keepdims=True), 1e-30)
            s_out[dest, chunk, :, here] = top
            q_out[dest, chunk, :, here] = (
                jnp.round(total * (LEVELS / top)).astype(jnp.int32).astype(jnp.int16)
            )
        for copy in hop(dest, way, chunk):
            copy.start()

    forward = jnp.where(lower, 0, 1)
    backward = 1 - forward

    def pass_forward(k):
        e = line - 1 - k
        dest = owner(e)

        @pl.when(u < e)
        def _():
            @pl.loop(0, chunks)
            def _(chunk):
                @pl.when(u > 0)
                def _():
                    take(dest, forward, chunk)

                give(dest, forward, chunk)

    def pass_backward(k):
        dest = owner(k)

        @pl.when(u > k)
        def _():
            @pl.loop(0, chunks)
            def _(chunk):
                take(dest, backward, chunk)
                give(dest, backward, chunk)

    own_vg().wait()
    pair_vg().wait_recv()
    multiply(order[0])
    pass_forward(0)
    for e in order[1:]:
        multiply(e)
    for k in range(1, line - 1):
        pass_forward(k)
        if k - 1 < line // 2 - 1:
            pass_backward(k - 1)

    norm_dp[dp] = jnp.zeros(norm_dp.shape[1:], F32)

    @pl.loop(0, chunks)
    def _(chunk):
        @pl.when(u > 0)
        def _():
            take(z, forward, chunk)

        take(z, backward, chunk)
        at = pl.ds(pl.multiple_of(chunk * part, part), part)
        for n in range(0, cols, tile):
            grad = acc[z, at, slice(n, n + tile)]
            square = jnp.sum((grad * grad).reshape(part // 8, 8, tile), axis=0)
            for lane in range(0, tile, 128):
                norm_dp[dp] += square[:, lane : lane + 128]

    def norm_to_dp(step):
        return pltpu.make_async_remote_copy(
            src_ref=norm_dp.at[dp],
            dst_ref=norm_dp.at[dp],
            send_sem=norm_dp_send.at[step],
            recv_sem=norm_dp_recv.at[step],
            device_id={"dp": lax.rem(dp + step, dpn)},
            device_id_type=MESH,
        )

    def norm_to_mp(step):
        return pltpu.make_async_remote_copy(
            src_ref=norm_mp.at[mp],
            dst_ref=norm_mp.at[mp],
            send_sem=norm_mp_send.at[step],
            recv_sem=norm_mp_recv.at[step],
            device_id={"mp": lax.rem(mp + step, heads)},
            device_id_type=MESH,
        )

    for step in range(1, dpn):
        norm_to_dp(step).start()
    for copy in loads:
        copy.wait()
    for step in range(1, dpn):
        norm_to_dp(step).wait_recv()
    norm_mp[mp] = jnp.sum(norm_dp[...], axis=0)
    for step in range(1, heads):
        norm_to_mp(step).start()
    for step in range(1, heads):
        norm_to_mp(step).wait_recv()
    square_sum = jnp.sum(jnp.sum(norm_mp[...], axis=0), keepdims=True)
    factor = jnp.minimum(1.0, clip_total / (jnp.sqrt(square_sum) + 1e-06))
    step_count = jnp.full((1, 1), step_ref[0].astype(F32), F32)
    scale_first, scale_second = adam_terms(step_count)

    def block(head, origin):
        return rollout_ref.at[pl.ds(pl.multiple_of((head * dpn + origin) * rows, rows), rows)]

    mine = pltpu.make_async_copy(update.at[mp], block(mp, dp), store_sem.at[3])

    def to_head(step):
        head = lax.rem(mp + step, heads)
        return pltpu.make_async_remote_copy(
            src_ref=update.at[head],
            dst_ref=block(mp, dp),
            send_sem=a2a_send.at[step],
            recv_sem=a2a_recv.at[step],
            device_id={"mp": head},
            device_id_type=MESH,
        )

    def relay(source, head, at_z, send, recv, to):
        return pltpu.make_async_remote_copy(
            src_ref=source,
            dst_ref=block(head, at_z * 2 + core),
            send_sem=send.at[at_z, head],
            recv_sem=recv.at[at_z, head],
            device_id={"dp": to},
            device_id_type=MESH,
        )

    def send_up(source, head, at_z):
        return relay(source, head, at_z, up_send, chain_recv, dp + 2)

    def send_down(source, head, at_z):
        return relay(source, head, at_z, down_send, chain_recv, dp - 2)

    def send_mate(source, head, at_z):
        return relay(source, head, at_z, mate_send, mate_recv, mate)

    def spread(source, head):
        @pl.when(z < line - 1)
        def _():
            send_up(source, head, z).start()

        @pl.when(z > 0)
        def _():
            send_down(source, head, z).start()

        send_mate(source, head, z).start()

    slab = min(32, rows)
    for step in range(heads):
        head = lax.rem(mp + step, heads)
        lanes = pl.ds(pl.multiple_of(head * head_cols, head_cols), head_cols)

        @pl.loop(0, rows // slab)
        def _(r):
            at = pl.ds(pl.multiple_of(r * slab, slab), slab)
            clipped = acc[z, at, lanes] * factor
            weight = w_in[at, lanes]
            first = 0.9 * m_in[at, lanes] + 0.1 * clipped
            second = 0.95 * v_in[at, lanes] + 0.05 * clipped * clipped
            m_out[at, lanes] = first
            v_out[at, lanes] = second
            direction = (first * scale_first) / (
                jnp.sqrt(second * scale_second) + 1e-08
            ) + 0.1 * weight
            w_out[at, lanes] = weight - 0.01 * direction
            update[head, at, :] = direction.astype(jnp.bfloat16)

        if step == 0:
            mine.start()
            spread(update.at[mp], mp)
        else:
            to_head(step).start()

    stores = [
        pltpu.make_async_copy(src, dst, store_sem.at[i])
        for i, (src, dst) in enumerate(
            ((w_out, new_master_ref), (m_out, new_first_ref), (v_out, new_second_ref))
        )
    ]
    for copy in stores:
        copy.start()

    for step in range(1, heads):
        head = lax.rem(mp + heads - step, heads)
        to_head(step).wait_recv()
        spread(block(head, dp), head)

    for far in range(1, line):
        for step in range(heads):
            head = lax.rem(mp + heads - step, heads)

            @pl.when(z - far >= 0)
            def _():
                at_z = z - far
                source = block(head, at_z * 2 + core)
                send_up(source, head, at_z).wait_recv()

                @pl.when(z < line - 1)
                def _():
                    send_up(source, head, at_z).start()

                send_mate(source, head, at_z).start()

            @pl.when(z + far < line)
            def _():
                at_z = z + far
                source = block(head, at_z * 2 + core)
                send_down(source, head, at_z).wait_recv()

                @pl.when(z > 0)
                def _():
                    send_down(source, head, at_z).start()

                send_mate(source, head, at_z).start()

    for at_z in range(line):
        for head in range(heads):
            source = block(head, at_z * 2 + core)
            send_mate(source, head, at_z).wait_recv()
            send_mate(source, head, at_z).wait_send()

            @pl.when((z < line - 1) & (z >= at_z))
            def _():
                send_up(source, head, at_z).wait_send()

            @pl.when((z > 0) & (z <= at_z))
            def _():
                send_down(source, head, at_z).wait_send()

    for step in range(1, heads):
        to_head(step).wait_send()
        norm_to_mp(step).wait_send()
    for step in range(1, dpn):
        norm_to_dp(step).wait_send()
    for dest in range(line):
        pair_act(dest).wait_send()

        @pl.when(z != dest)
        def _():
            @pl.loop(0, chunks)
            def _(chunk):
                for copy in hop(dest, 0, chunk):
                    copy.wait_send()

    pair_vg().wait_send()
    mine.wait()
    for copy in stores:
        copy.wait()


def one_kernel(line, heads, activations, value_grad, master, first_moment, second_moment, step_count):
    rows, cols = master.shape
    tokens = activations.shape[0]
    chunks = 4
    part = rows // chunks
    dpn = 2 * line
    clip_total = 0.5 * math.sqrt(rows * dpn * heads * cols)
    hbm = pl.BlockSpec(memory_space=pl.ANY)
    owned = jax.ShapeDtypeStruct((rows, cols), F32)
    wide = pltpu.VMEM((rows, cols), F32)
    dma = pltpu.SemaphoreType.DMA
    return pl.pallas_call(
        functools.partial(kernel, line, heads, chunks, clip_total),
        out_shape=(
            owned,
            owned,
            owned,
            jax.ShapeDtypeStruct((rows * dpn * heads, cols // heads), jnp.bfloat16),
        ),
        in_specs=[pl.BlockSpec(memory_space=pltpu.SMEM)] + [hbm] * 5,
        out_specs=(hbm,) * 4,
        scratch_shapes=[
            pltpu.VMEM((line, 2 * tokens, rows), jnp.bfloat16),
            pltpu.VMEM((2 * tokens, cols), jnp.bfloat16),
            pltpu.VMEM((line, rows, cols), F32),
            pltpu.VMEM((line, chunks, part, cols), jnp.int16),
            pltpu.VMEM((line, chunks, 1, cols), F32),
            pltpu.VMEM((2, line, chunks, part, cols), jnp.int16),
            pltpu.VMEM((2, line, chunks, 1, cols), F32),
            pltpu.VMEM((dpn, 8, 128), F32),
            pltpu.VMEM((heads, 8, 128), F32),
            wide,
            wide,
            wide,
            wide,
            wide,
            wide,
            pltpu.VMEM((heads, rows, cols // heads), jnp.bfloat16),
            dma((line + 1,)),
            dma((line + 1,)),
            dma((line + 1,)),
            dma((3,)),
            dma((2, line, chunks)),
            dma((2, 2, line, chunks)),
            dma((dpn,)),
            dma((dpn,)),
            dma((heads,)),
            dma((heads,)),
            dma((4,)),
            dma((heads,)),
            dma((heads,)),
            dma((line, heads)),
            dma((line, heads)),
            dma((line, heads)),
            dma((line, heads)),
            dma((line, heads)),
        ],
        compiler_params=pltpu.CompilerParams(
            collective_id=0, has_side_effects=True, vmem_limit_bytes=48 * 1024 * 1024
        ),
    )(step_count, activations, value_grad, master, first_moment, second_moment)


def plain(activations, value_grad, master, first_moment, second_moment, step_count):
    own_rows, cols = master.shape
    grad = lax.psum_scatter(
        lax.dot_general(
            activations, value_grad, (((0,), (0,)), ((), ())), preferred_element_type=F32
        ),
        "dp",
        scatter_dimension=0,
        tiled=True,
    )
    square_sum = lax.psum(jnp.sum(grad * grad), ("dp", "mp"))
    head_count = lax.axis_size("mp")
    clip_total = 0.5 * math.sqrt(own_rows * lax.axis_size("dp") * head_count * cols)
    factor = jnp.minimum(jnp.float32(1.0), clip_total / (jnp.sqrt(square_sum) + 1e-06))
    clipped = factor * grad
    new_first = 0.9 * first_moment + 0.1 * clipped
    new_second = 0.95 * second_moment + 0.05 * clipped * clipped
    scale_first, scale_second = adam_terms(step_count[0].astype(F32))
    direction = new_first * scale_first / (jnp.sqrt(new_second * scale_second) + 1e-08) + 0.1 * master
    new_master = master - 0.01 * direction
    update = direction.astype(jnp.bfloat16)
    received = lax.all_to_all(update, "mp", split_axis=1, concat_axis=0, tiled=True)
    stacked = received.reshape(head_count, own_rows, received.shape[1])
    gathered = lax.all_gather(stacked, "dp", axis=1, tiled=True)
    return (new_master, new_first, new_second, gathered.reshape(-1, gathered.shape[2]))


def solution(mesh):
    dpn, heads = mesh.shape["dp"], mesh.shape["mp"]

    def on_device(*args):
        rows, cols = args[2].shape
        if dpn % 4 == 0 and dpn <= 16 and rows % 128 == 0 and (cols // heads) % 128 == 0:
            return one_kernel(dpn // 2, heads, *args)
        return plain(*args)

    in_specs = (
        P("dp", "mp"),
        P("dp", None),
        P(("mp", "dp"), None),
        P(("mp", "dp"), None),
        P(("mp", "dp"), None),
        P(),
    )
    out_specs = (P(("mp", "dp"), None), P(("mp", "dp"), None), P(("mp", "dp"), None), P(None, "mp"))
    return jax.shard_map(
        on_device, mesh=mesh, in_specs=in_specs, out_specs=out_specs, check_vma=False
    )
```

```python
import functools
import math

import jax
import jax.numpy as jnp
from jax import lax
from jax.experimental import pallas as pl
from jax.experimental.pallas import tpu as pltpu
from jax.sharding import PartitionSpec as P

F32 = jnp.float32
LEVELS = 32760.0
PIECES = (1, 1, 1, 4)
MESH = pl.DeviceIdType.MESH


def adam_terms(step):
    bias_first = 1.0 - jnp.exp(step * jnp.float32(math.log(0.9)))
    bias_second = 1.0 - jnp.exp(step * jnp.float32(math.log(0.95)))
    return 1.0 / bias_first, 1.0 / bias_second


def kernel(
    line,
    heads,
    chunks,
    clip_total,
    step_ref,
    act_ref,
    vg_ref,
    master_ref,
    first_ref,
    second_ref,
    new_master_ref,
    new_first_ref,
    new_second_ref,
    rollout_ref,
    act,
    vg,
    acc,
    q_out,
    s_out,
    q_in,
    s_in,
    norm_dp,
    norm_mp,
    w_in,
    m_in,
    v_in,
    w_out,
    m_out,
    v_out,
    update,
    in_sem,
    pair_send,
    pair_recv,
    load_sem,
    rs_send,
    rs_recv,
    norm_dp_send,
    norm_dp_recv,
    norm_mp_send,
    norm_mp_recv,
    store_sem,
    a2a_send,
    a2a_recv,
    up_send,
    down_send,
    chain_recv,
    mate_send,
    mate_recv,
):
    dpn = 2 * line
    dp = lax.axis_index("dp")
    mp = lax.axis_index("mp")
    z = dp // 2
    core = lax.rem(dp, 2)
    mate = dp + 1 - 2 * core
    tokens = act_ref.shape[0]
    rows = master_ref.shape[0]
    cols = master_ref.shape[1]
    tile = cols // chunks
    group = rows // 8
    head_cols = cols // heads

    barrier = pltpu.get_barrier_semaphore()
    for step in range(1, dpn):
        pl.semaphore_signal(
            barrier, inc=1, device_id={"dp": lax.rem(dp + step, dpn)}, device_id_type=MESH
        )
    for step in range(1, heads):
        pl.semaphore_signal(
            barrier, inc=1, device_id={"mp": lax.rem(mp + step, heads)}, device_id_type=MESH
        )

    lower = z < line // 2
    def owner(e):
        return jnp.where(lower, e, line - 1 - e)

    u = jnp.where(lower, z, line - 1 - z)

    def own_act(e):
        dest = owner(e)
        start = pl.multiple_of((dest * 2 + core) * rows, rows)
        return pltpu.make_async_copy(
            act_ref.at[:, pl.ds(start, rows)],
            act.at[dest, pl.ds(0, tokens)],
            in_sem.at[dest],
        )

    def own_vg(n):
        at = slice(n * tile, (n + 1) * tile)
        return pltpu.make_async_copy(
            vg_ref.at[:, at], vg.at[pl.ds(0, tokens), at], in_sem.at[line + n]
        )

    def pair_act(e):
        dest = owner(e)
        start = pl.multiple_of((dest * 2 + 1 - core) * rows, rows)
        return pltpu.make_async_remote_copy(
            src_ref=act_ref.at[:, pl.ds(start, rows)],
            dst_ref=act.at[dest, pl.ds(tokens, tokens)],
            send_sem=pair_send.at[dest],
            recv_sem=pair_recv.at[dest],
            device_id={"dp": mate},
            device_id_type=MESH,
        )

    def pair_vg(n):
        at = slice(n * tile, (n + 1) * tile)
        return pltpu.make_async_remote_copy(
            src_ref=vg_ref.at[:, at],
            dst_ref=vg.at[pl.ds(tokens, tokens), at],
            send_sem=pair_send.at[line + n],
            recv_sem=pair_recv.at[line + n],
            device_id={"dp": mate},
            device_id_type=MESH,
        )

    order = list(range(line - 1, -1, -1))
    own_act(order[0]).start()
    for n in range(chunks):
        own_vg(n).start()
    for e in order[1:]:
        own_act(e).start()
    loads = [
        pltpu.make_async_copy(src, dst, load_sem.at[i])
        for i, (src, dst) in enumerate(
            ((master_ref, w_in), (first_ref, m_in), (second_ref, v_in))
        )
    ]
    pl.semaphore_wait(barrier, dpn - 1 + heads - 1)
    pair_act(order[0]).start()
    for n in range(chunks):
        pair_vg(n).start()
    for e in order[1:]:
        pair_act(e).start()
    for copy in loads:
        copy.start()

    def multiply(dest, n):
        at = pl.ds(pl.multiple_of(n * tile, tile), tile)
        acc[dest, :, at] = lax.dot_general(
            act[dest], vg[:, at], (((0,), (0,)), ((), ())), preferred_element_type=F32
        )

    def hop(dest, way, chunk):
        to = (z + 1 - 2 * way) * 2 + core
        data = pltpu.make_async_remote_copy(
            src_ref=q_out.at[dest, chunk],
            dst_ref=q_in.at[way, dest, chunk],
            send_sem=rs_send.at[0, dest, chunk],
            recv_sem=rs_recv.at[0, way, dest, chunk],
            device_id={"dp": to},
            device_id_type=MESH,
        )
        scale = pltpu.make_async_remote_copy(
            src_ref=s_out.at[dest, chunk],
            dst_ref=s_in.at[way, dest, chunk],
            send_sem=rs_send.at[1, dest, chunk],
            recv_sem=rs_recv.at[1, way, dest, chunk],
            device_id={"dp": to},
            device_id_type=MESH,
        )
        return data, scale

    def take(dest, way, chunk):
        for copy in hop(dest, way, chunk):
            copy.wait_recv()
        lanes = pl.ds(pl.multiple_of(chunk * tile, tile), tile)
        for g in range(8):
            here = slice(g * group, (g + 1) * group)
            got = q_in[way, dest, chunk, here, :].astype(jnp.int32).astype(F32)
            top = s_in[way, dest, chunk, slice(g, g + 1), :]
            acc[dest, here, lanes] += got * (top * (1.0 / LEVELS))

    def give(dest, way, chunk):
        lanes = pl.ds(pl.multiple_of(chunk * tile, tile), tile)
        for g in range(8):
            here = slice(g * group, (g + 1) * group)
            total = acc[dest, here, lanes]
            top = jnp.maximum(jnp.max(jnp.abs(total), axis=0, keepdims=True), 1e-30)
            s_out[dest, chunk, slice(g, g + 1), :] = top
            q_out[dest, chunk, here, :] = (
                jnp.round(total * (LEVELS / top)).astype(jnp.int32).astype(jnp.int16)
            )
        for copy in hop(dest, way, chunk):
            copy.start()

    forward = jnp.where(lower, 0, 1)
    backward = 1 - forward

    def pass_forward(k):
        e = line - 1 - k
        dest = owner(e)

        @pl.when(u < e)
        def _():
            @pl.loop(0, chunks)
            def _(chunk):
                @pl.when(u > 0)
                def _():
                    take(dest, forward, chunk)

                give(dest, forward, chunk)

    def pass_backward(k):
        dest = owner(k)

        @pl.when(u > k)
        def _():
            @pl.loop(0, chunks)
            def _(chunk):
                take(dest, backward, chunk)
                give(dest, backward, chunk)

    far = owner(line - 1)
    own_act(line - 1).wait()
    pair_act(line - 1).wait_recv()
    for n in range(chunks):
        own_vg(n).wait()
        pair_vg(n).wait_recv()
        multiply(far, n)

        @pl.when(u == 0)
        def _():
            give(far, forward, n)

    for e in order[1:]:
        own_act(e).wait()
        pair_act(e).wait_recv()

        @pl.loop(0, chunks)
        def _(n):
            multiply(owner(e), n)

    @pl.when(u > 0)
    def _():
        pass_forward(0)

    for k in range(1, line - 1):
        pass_forward(k)
        if k - 1 < line // 2 - 1:
            pass_backward(k - 1)

    norm_dp[dp] = jnp.zeros(norm_dp.shape[1:], F32)

    @pl.loop(0, chunks)
    def _(chunk):
        @pl.when(u > 0)
        def _():
            take(z, forward, chunk)

        take(z, backward, chunk)
        lanes = pl.ds(pl.multiple_of(chunk * tile, tile), tile)
        square = jnp.zeros((8, tile), F32)
        for g in range(8):
            grad = acc[z, slice(g * group, (g + 1) * group), lanes]
            square += jnp.sum((grad * grad).reshape(group // 8, 8, tile), axis=0)
        for lane in range(0, tile, 128):
            norm_dp[dp] += square[:, lane : lane + 128]

    def norm_to_dp(step):
        return pltpu.make_async_remote_copy(
            src_ref=norm_dp.at[dp],
            dst_ref=norm_dp.at[dp],
            send_sem=norm_dp_send.at[step],
            recv_sem=norm_dp_recv.at[step],
            device_id={"dp": lax.rem(dp + step, dpn)},
            device_id_type=MESH,
        )

    def norm_to_mp(step):
        return pltpu.make_async_remote_copy(
            src_ref=norm_mp.at[mp],
            dst_ref=norm_mp.at[mp],
            send_sem=norm_mp_send.at[step],
            recv_sem=norm_mp_recv.at[step],
            device_id={"mp": lax.rem(mp + step, heads)},
            device_id_type=MESH,
        )

    for step in range(1, dpn):
        norm_to_dp(step).start()
    for copy in loads:
        copy.wait()
    for step in range(1, dpn):
        norm_to_dp(step).wait_recv()
    norm_mp[mp] = jnp.sum(norm_dp[...], axis=0)
    for step in range(1, heads):
        norm_to_mp(step).start()
    for step in range(1, heads):
        norm_to_mp(step).wait_recv()
    square_sum = jnp.sum(jnp.sum(norm_mp[...], axis=0), keepdims=True)
    factor = jnp.minimum(1.0, clip_total / (jnp.sqrt(square_sum) + 1e-06))
    step_count = jnp.full((1, 1), step_ref[0].astype(F32), F32)
    scale_first, scale_second = adam_terms(step_count)

    def block(head, origin):
        return rollout_ref.at[pl.ds(pl.multiple_of((head * dpn + origin) * rows, rows), rows)]

    mine = pltpu.make_async_copy(update.at[mp], block(mp, dp), store_sem.at[3])

    def to_head(step):
        head = lax.rem(mp + step, heads)
        return pltpu.make_async_remote_copy(
            src_ref=update.at[head],
            dst_ref=block(mp, dp),
            send_sem=a2a_send.at[step],
            recv_sem=a2a_recv.at[step],
            device_id={"mp": head},
            device_id_type=MESH,
        )

    def relay(source, head, at_z, send, recv, to):
        return pltpu.make_async_remote_copy(
            src_ref=source,
            dst_ref=block(head, at_z * 2 + core),
            send_sem=send.at[at_z, head],
            recv_sem=recv.at[at_z, head],
            device_id={"dp": to},
            device_id_type=MESH,
        )

    def send_up(source, head, at_z):
        return relay(source, head, at_z, up_send, chain_recv, dp + 2)

    def send_down(source, head, at_z):
        return relay(source, head, at_z, down_send, chain_recv, dp - 2)

    def send_mate(source, head, at_z):
        return relay(source, head, at_z, mate_send, mate_recv, mate)

    def spread(source, head):
        @pl.when(z < line - 1)
        def _():
            send_up(source, head, z).start()

        @pl.when(z > 0)
        def _():
            send_down(source, head, z).start()

        send_mate(source, head, z).start()

    slab = min(32, rows)
    for step in (*range(1, heads), 0):
        head = lax.rem(mp + step, heads)
        lanes = pl.ds(pl.multiple_of(head * head_cols, head_cols), head_cols)

        @pl.loop(0, rows // slab)
        def _(r):
            at = pl.ds(pl.multiple_of(r * slab, slab), slab)
            clipped = acc[z, at, lanes] * factor
            weight = w_in[at, lanes]
            first = 0.9 * m_in[at, lanes] + 0.1 * clipped
            second = 0.95 * v_in[at, lanes] + 0.05 * clipped * clipped
            m_out[at, lanes] = first
            v_out[at, lanes] = second
            direction = (first * scale_first) / (
                jnp.sqrt(second * scale_second) + 1e-08
            ) + 0.1 * weight
            w_out[at, lanes] = weight - 0.01 * direction
            update[head, at, :] = direction.astype(jnp.bfloat16)

        if step == 0:
            mine.start()
            spread(update.at[mp], mp)
        else:
            to_head(step).start()

    stores = [
        pltpu.make_async_copy(src, dst, store_sem.at[i])
        for i, (src, dst) in enumerate(
            ((w_out, new_master_ref), (m_out, new_first_ref), (v_out, new_second_ref))
        )
    ]
    for copy in stores:
        copy.start()

    for step in range(1, heads):
        head = lax.rem(mp + heads - step, heads)
        to_head(step).wait_recv()
        spread(block(head, dp), head)

    for far in range(1, line):
        for step in range(heads):
            head = lax.rem(mp + heads - step, heads)

            @pl.when(z - far >= 0)
            def _():
                at_z = z - far
                source = block(head, at_z * 2 + core)
                send_up(source, head, at_z).wait_recv()

                @pl.when(z < line - 1)
                def _():
                    send_up(source, head, at_z).start()

                send_mate(source, head, at_z).start()

            @pl.when(z + far < line)
            def _():
                at_z = z + far
                source = block(head, at_z * 2 + core)
                send_down(source, head, at_z).wait_recv()

                @pl.when(z > 0)
                def _():
                    send_down(source, head, at_z).start()

                send_mate(source, head, at_z).start()

    for at_z in range(line):
        for head in range(heads):
            source = block(head, at_z * 2 + core)
            send_mate(source, head, at_z).wait_recv()
            send_mate(source, head, at_z).wait_send()

            @pl.when((z < line - 1) & (z >= at_z))
            def _():
                send_up(source, head, at_z).wait_send()

            @pl.when((z > 0) & (z <= at_z))
            def _():
                send_down(source, head, at_z).wait_send()

    for step in range(1, heads):
        to_head(step).wait_send()
        norm_to_mp(step).wait_send()
    for step in range(1, dpn):
        norm_to_dp(step).wait_send()
    for dest in range(line):
        pair_act(dest).wait_send()

        @pl.when(z != dest)
        def _():
            @pl.loop(0, chunks)
            def _(chunk):
                for copy in hop(dest, 0, chunk):
                    copy.wait_send()

    for n in range(chunks):
        pair_vg(n).wait_send()
    mine.wait()
    for copy in stores:
        copy.wait()


def settle(*refs):
    count = (len(refs) - 1) // 2
    sem = refs[-1]
    copies = []
    for i in range(count):
        source, place = refs[i], refs[count + i]
        piece = source.shape[0] // PIECES[i]
        for j in range(PIECES[i]):
            at = pl.ds(j * piece, piece)
            copies.append(
                pltpu.make_async_copy(source.at[at], place.at[at], sem.at[len(copies)])
            )
    for copy in copies:
        copy.start()
    for copy in copies:
        copy.wait()


def one_kernel(line, heads, activations, value_grad, master, first_moment, second_moment, step_count):
    rows, cols = master.shape
    tokens = activations.shape[0]
    chunks = 4
    dpn = 2 * line
    clip_total = 0.5 * math.sqrt(rows * dpn * heads * cols)
    hbm = pl.BlockSpec(memory_space=pl.ANY)
    owned = jax.ShapeDtypeStruct((rows, cols), F32)
    wide = pltpu.VMEM((rows, cols), F32)
    dma = pltpu.SemaphoreType.DMA
    results = pl.pallas_call(
        functools.partial(kernel, line, heads, chunks, clip_total),
        out_shape=(
            owned,
            owned,
            owned,
            jax.ShapeDtypeStruct((rows * dpn * heads, cols // heads), jnp.bfloat16),
        ),
        in_specs=[pl.BlockSpec(memory_space=pltpu.SMEM)]
        + [hbm] * 5,
        out_specs=(hbm,) * 4,
        scratch_shapes=[
            pltpu.VMEM((line, 2 * tokens, rows), jnp.bfloat16),
            pltpu.VMEM((2 * tokens, cols), jnp.bfloat16),
            pltpu.VMEM((line, rows, cols), F32),
            pltpu.VMEM((line, chunks, rows, cols // chunks), jnp.int16),
            pltpu.VMEM((line, chunks, 8, cols // chunks), F32),
            pltpu.VMEM((2, line, chunks, rows, cols // chunks), jnp.int16),
            pltpu.VMEM((2, line, chunks, 8, cols // chunks), F32),
            pltpu.VMEM((dpn, 8, 128), F32),
            pltpu.VMEM((heads, 8, 128), F32),
            wide,
            wide,
            wide,
            wide,
            wide,
            wide,
            pltpu.VMEM((heads, rows, cols // heads), jnp.bfloat16),
            dma((line + chunks,)),
            dma((line + chunks,)),
            dma((line + chunks,)),
            dma((3,)),
            dma((2, line, chunks)),
            dma((2, 2, line, chunks)),
            dma((dpn,)),
            dma((dpn,)),
            dma((heads,)),
            dma((heads,)),
            dma((4,)),
            dma((heads,)),
            dma((heads,)),
            dma((line, heads)),
            dma((line, heads)),
            dma((line, heads)),
            dma((line, heads)),
            dma((line, heads)),
        ],
        compiler_params=pltpu.CompilerParams(
            collective_id=0, has_side_effects=True, vmem_limit_bytes=28 * 1024 * 1024
        ),
    )(
        step_count,
        *(
            pltpu.with_memory_space_constraint(x, pltpu.HBM)
            for x in (activations, value_grad, master, first_moment, second_moment)
        ),
    )
    shapes = tuple(jax.ShapeDtypeStruct(x.shape, x.dtype) for x in results)
    return pl.pallas_call(
        settle,
        out_shape=shapes,
        in_specs=[hbm] * 4,
        out_specs=(hbm,) * 4,
        scratch_shapes=[dma((sum(PIECES),))],
        compiler_params=pltpu.CompilerParams(vmem_limit_bytes=4 * 1024 * 1024),
    )(*(pltpu.with_memory_space_constraint(x, pltpu.VMEM) for x in results))


def plain(activations, value_grad, master, first_moment, second_moment, step_count):
    own_rows, cols = master.shape
    grad = lax.psum_scatter(
        lax.dot_general(
            activations, value_grad, (((0,), (0,)), ((), ())), preferred_element_type=F32
        ),
        "dp",
        scatter_dimension=0,
        tiled=True,
    )
    square_sum = lax.psum(jnp.sum(grad * grad), ("dp", "mp"))
    head_count = lax.axis_size("mp")
    clip_total = 0.5 * math.sqrt(own_rows * lax.axis_size("dp") * head_count * cols)
    factor = jnp.minimum(jnp.float32(1.0), clip_total / (jnp.sqrt(square_sum) + 1e-06))
    clipped = factor * grad
    new_first = 0.9 * first_moment + 0.1 * clipped
    new_second = 0.95 * second_moment + 0.05 * clipped * clipped
    scale_first, scale_second = adam_terms(step_count[0].astype(F32))
    direction = new_first * scale_first / (jnp.sqrt(new_second * scale_second) + 1e-08) + 0.1 * master
    new_master = master - 0.01 * direction
    update = direction.astype(jnp.bfloat16)
    received = lax.all_to_all(update, "mp", split_axis=1, concat_axis=0, tiled=True)
    stacked = received.reshape(head_count, own_rows, received.shape[1])
    gathered = lax.all_gather(stacked, "dp", axis=1, tiled=True)
    return (new_master, new_first, new_second, gathered.reshape(-1, gathered.shape[2]))


def solution(mesh):
    dpn, heads = mesh.shape["dp"], mesh.shape["mp"]

    def on_device(*args):
        rows, cols = args[2].shape
        if dpn % 4 == 0 and dpn <= 16 and rows % 128 == 0 and (cols // heads) % 128 == 0:
            return one_kernel(dpn // 2, heads, *args)
        return plain(*args)

    in_specs = (
        P("dp", "mp"),
        P("dp", None),
        P(("mp", "dp"), None),
        P(("mp", "dp"), None),
        P(("mp", "dp"), None),
        P(),
    )
    out_specs = (P(("mp", "dp"), None), P(("mp", "dp"), None), P(("mp", "dp"), None), P(None, "mp"))
    return jax.shard_map(
        on_device, mesh=mesh, in_specs=in_specs, out_specs=out_specs, check_vma=False
    )
```

```python
import functools
import math

import jax
import jax.numpy as jnp
from jax import lax
from jax.experimental import pallas as pl
from jax.experimental.pallas import tpu as pltpu
from jax.sharding import PartitionSpec as P

F32 = jnp.float32
LEVELS = 32760.0
PIECES = (1, 1, 1, 4)
MESH = pl.DeviceIdType.MESH


def adam_terms(step):
    bias_first = 1.0 - jnp.exp(step * jnp.float32(math.log(0.9)))
    bias_second = 1.0 - jnp.exp(step * jnp.float32(math.log(0.95)))
    return 1.0 / bias_first, 1.0 / bias_second


def kernel(
    line,
    heads,
    chunks,
    clip_total,
    step_ref,
    act_ref,
    vg_ref,
    master_ref,
    first_ref,
    second_ref,
    new_master_ref,
    new_first_ref,
    new_second_ref,
    rollout_ref,
    act,
    vg,
    acc,
    q_out,
    s_out,
    q_in,
    s_in,
    norm_dp,
    norm_mp,
    w_in,
    m_in,
    v_in,
    w_out,
    m_out,
    v_out,
    update,
    in_sem,
    pair_send,
    pair_recv,
    load_sem,
    rs_send,
    rs_recv,
    norm_dp_send,
    norm_dp_recv,
    norm_mp_send,
    norm_mp_recv,
    store_sem,
    a2a_send,
    a2a_recv,
    up_send,
    down_send,
    chain_recv,
    mate_send,
    mate_recv,
):
    dpn = 2 * line
    dp = lax.axis_index("dp")
    mp = lax.axis_index("mp")
    z = dp // 2
    core = lax.rem(dp, 2)
    mate = dp + 1 - 2 * core
    tokens = act_ref.shape[0]
    rows = master_ref.shape[0]
    cols = master_ref.shape[1]
    tile = cols // chunks
    group = rows // 8
    head_cols = cols // heads

    barrier = pltpu.get_barrier_semaphore()
    for step in range(1, dpn):
        pl.semaphore_signal(
            barrier, inc=1, device_id={"dp": lax.rem(dp + step, dpn)}, device_id_type=MESH
        )
    for step in range(1, heads):
        pl.semaphore_signal(
            barrier, inc=1, device_id={"mp": lax.rem(mp + step, heads)}, device_id_type=MESH
        )

    lower = z < line // 2
    def owner(e):
        return jnp.where(lower, e, line - 1 - e)

    u = jnp.where(lower, z, line - 1 - z)

    def own_act(e):
        dest = owner(e)
        start = pl.multiple_of((dest * 2 + core) * rows, rows)
        return pltpu.make_async_copy(
            act_ref.at[:, pl.ds(start, rows)],
            act.at[dest, pl.ds(0, tokens)],
            in_sem.at[dest],
        )

    def own_vg(n):
        at = slice(n * tile, (n + 1) * tile)
        return pltpu.make_async_copy(
            vg_ref.at[:, at], vg.at[pl.ds(0, tokens), at], in_sem.at[line + n]
        )

    def pair_act(e):
        dest = owner(e)
        start = pl.multiple_of((dest * 2 + 1 - core) * rows, rows)
        return pltpu.make_async_remote_copy(
            src_ref=act_ref.at[:, pl.ds(start, rows)],
            dst_ref=act.at[dest, pl.ds(tokens, tokens)],
            send_sem=pair_send.at[dest],
            recv_sem=pair_recv.at[dest],
            device_id={"dp": mate},
            device_id_type=MESH,
        )

    def pair_vg(n):
        at = slice(n * tile, (n + 1) * tile)
        return pltpu.make_async_remote_copy(
            src_ref=vg_ref.at[:, at],
            dst_ref=vg.at[pl.ds(tokens, tokens), at],
            send_sem=pair_send.at[line + n],
            recv_sem=pair_recv.at[line + n],
            device_id={"dp": mate},
            device_id_type=MESH,
        )

    order = list(range(line - 1, -1, -1))
    own_act(order[0]).start()
    for n in range(chunks):
        own_vg(n).start()
    for e in order[1:]:
        own_act(e).start()
    loads = [
        pltpu.make_async_copy(src, dst, load_sem.at[i])
        for i, (src, dst) in enumerate(
            ((master_ref, w_in), (first_ref, m_in), (second_ref, v_in))
        )
    ]
    pl.semaphore_wait(barrier, dpn - 1 + heads - 1)
    pair_act(order[0]).start()
    for n in range(chunks):
        pair_vg(n).start()
    for e in order[1:]:
        pair_act(e).start()
    for copy in loads:
        copy.start()

    def multiply(dest, n):
        at = pl.ds(pl.multiple_of(n * tile, tile), tile)
        acc[dest, :, at] = lax.dot_general(
            act[dest], vg[:, at], (((0,), (0,)), ((), ())), preferred_element_type=F32
        )

    def hop(dest, way, chunk):
        to = (z + 1 - 2 * way) * 2 + core
        data = pltpu.make_async_remote_copy(
            src_ref=q_out.at[dest, chunk],
            dst_ref=q_in.at[way, dest, chunk],
            send_sem=rs_send.at[0, dest, chunk],
            recv_sem=rs_recv.at[0, way, dest, chunk],
            device_id={"dp": to},
            device_id_type=MESH,
        )
        scale = pltpu.make_async_remote_copy(
            src_ref=s_out.at[dest, chunk],
            dst_ref=s_in.at[way, dest, chunk],
            send_sem=rs_send.at[1, dest, chunk],
            recv_sem=rs_recv.at[1, way, dest, chunk],
            device_id={"dp": to},
            device_id_type=MESH,
        )
        return data, scale

    def take(dest, way, chunk):
        for copy in hop(dest, way, chunk):
            copy.wait_recv()
        lanes = pl.ds(pl.multiple_of(chunk * tile, tile), tile)
        top = s_in[way, dest, chunk] * (1.0 / LEVELS)
        for g in range(8):
            here = slice(g * group, (g + 1) * group)
            got = q_in[way, dest, chunk, here, :].astype(jnp.int32).astype(F32)
            acc[dest, here, lanes] += got * top

    def give(dest, way, chunk):
        lanes = pl.ds(pl.multiple_of(chunk * tile, tile), tile)
        peak = jnp.zeros((8, tile), F32)
        for g in range(rows // 8):
            peak = jnp.maximum(peak, jnp.abs(acc[dest, slice(g * 8, (g + 1) * 8), lanes]))
        top = jnp.maximum(jnp.max(peak, axis=0, keepdims=True), 1e-30)
        s_out[dest, chunk] = top
        ratio = LEVELS / top
        for g in range(8):
            here = slice(g * group, (g + 1) * group)
            total = acc[dest, here, lanes]
            q_out[dest, chunk, here, :] = (
                jnp.round(total * ratio).astype(jnp.int32).astype(jnp.int16)
            )
        for copy in hop(dest, way, chunk):
            copy.start()

    forward = jnp.where(lower, 0, 1)
    backward = 1 - forward

    def pass_forward(k):
        e = line - 1 - k
        dest = owner(e)

        @pl.when(u < e)
        def _():
            @pl.loop(0, chunks)
            def _(chunk):
                @pl.when(u > 0)
                def _():
                    take(dest, forward, chunk)

                give(dest, forward, chunk)

    def pass_backward(k):
        dest = owner(k)

        @pl.when(u > k)
        def _():
            @pl.loop(0, chunks)
            def _(chunk):
                take(dest, backward, chunk)
                give(dest, backward, chunk)

    far = owner(line - 1)
    own_act(line - 1).wait()
    pair_act(line - 1).wait_recv()
    for n in range(chunks):
        own_vg(n).wait()
        pair_vg(n).wait_recv()
        multiply(far, n)

        @pl.when(u == 0)
        def _():
            give(far, forward, n)

    for e in order[1:]:
        own_act(e).wait()
        pair_act(e).wait_recv()

        @pl.loop(0, chunks)
        def _(n):
            multiply(owner(e), n)

    @pl.when(u > 0)
    def _():
        pass_forward(0)

    for k in range(1, line - 1):
        pass_forward(k)
        if k - 1 < line // 2 - 1:
            pass_backward(k - 1)

    norm_dp[dp] = jnp.zeros(norm_dp.shape[1:], F32)

    @pl.loop(0, chunks)
    def _(chunk):
        take(z, backward, chunk)

        @pl.when(u > 0)
        def _():
            take(z, forward, chunk)

        lanes = pl.ds(pl.multiple_of(chunk * tile, tile), tile)
        square = jnp.zeros((8, tile), F32)
        for g in range(8):
            grad = acc[z, slice(g * group, (g + 1) * group), lanes]
            square += jnp.sum((grad * grad).reshape(group // 8, 8, tile), axis=0)
        for lane in range(0, tile, 128):
            norm_dp[dp] += square[:, lane : lane + 128]

    def norm_to_dp(step):
        return pltpu.make_async_remote_copy(
            src_ref=norm_dp.at[dp],
            dst_ref=norm_dp.at[dp],
            send_sem=norm_dp_send.at[step],
            recv_sem=norm_dp_recv.at[step],
            device_id={"dp": lax.rem(dp + step, dpn)},
            device_id_type=MESH,
        )

    def norm_to_mp(step):
        return pltpu.make_async_remote_copy(
            src_ref=norm_mp.at[mp],
            dst_ref=norm_mp.at[mp],
            send_sem=norm_mp_send.at[step],
            recv_sem=norm_mp_recv.at[step],
            device_id={"mp": lax.rem(mp + step, heads)},
            device_id_type=MESH,
        )

    for step in range(1, dpn):
        norm_to_dp(step).start()
    for copy in loads:
        copy.wait()
    for step in range(1, dpn):
        norm_to_dp(step).wait_recv()
    norm_mp[mp] = jnp.sum(norm_dp[...], axis=0)
    for step in range(1, heads):
        norm_to_mp(step).start()
    for step in range(1, heads):
        norm_to_mp(step).wait_recv()
    square_sum = jnp.sum(jnp.sum(norm_mp[...], axis=0), keepdims=True)
    factor = jnp.minimum(1.0, clip_total / (jnp.sqrt(square_sum) + 1e-06))
    step_count = jnp.full((1, 1), step_ref[0].astype(F32), F32)
    scale_first, scale_second = adam_terms(step_count)

    def block(head, origin):
        return rollout_ref.at[pl.ds(pl.multiple_of((head * dpn + origin) * rows, rows), rows)]

    mine = pltpu.make_async_copy(update.at[mp], block(mp, dp), store_sem.at[3])

    def to_head(step):
        head = lax.rem(mp + step, heads)
        return pltpu.make_async_remote_copy(
            src_ref=update.at[head],
            dst_ref=block(mp, dp),
            send_sem=a2a_send.at[step],
            recv_sem=a2a_recv.at[step],
            device_id={"mp": head},
            device_id_type=MESH,
        )

    def relay(source, head, at_z, send, recv, to):
        return pltpu.make_async_remote_copy(
            src_ref=source,
            dst_ref=block(head, at_z * 2 + core),
            send_sem=send.at[at_z, head],
            recv_sem=recv.at[at_z, head],
            device_id={"dp": to},
            device_id_type=MESH,
        )

    def send_up(source, head, at_z):
        return relay(source, head, at_z, up_send, chain_recv, dp + 2)

    def send_down(source, head, at_z):
        return relay(source, head, at_z, down_send, chain_recv, dp - 2)

    def send_mate(source, head, at_z):
        return relay(source, head, at_z, mate_send, mate_recv, mate)

    def spread(source, head):
        @pl.when(z < line - 1)
        def _():
            send_up(source, head, z).start()

        @pl.when(z > 0)
        def _():
            send_down(source, head, z).start()

        send_mate(source, head, z).start()

    slab = min(32, rows)
    for step in (*range(1, heads), 0):
        head = lax.rem(mp + step, heads)
        lanes = pl.ds(pl.multiple_of(head * head_cols, head_cols), head_cols)

        @pl.loop(0, rows // slab)
        def _(r):
            at = pl.ds(pl.multiple_of(r * slab, slab), slab)
            clipped = acc[z, at, lanes] * factor
            weight = w_in[at, lanes]
            first = 0.9 * m_in[at, lanes] + 0.1 * clipped
            second = 0.95 * v_in[at, lanes] + 0.05 * clipped * clipped
            m_out[at, lanes] = first
            v_out[at, lanes] = second
            direction = (first * scale_first) / (
                jnp.sqrt(second * scale_second) + 1e-08
            ) + 0.1 * weight
            w_out[at, lanes] = weight - 0.01 * direction
            update[head, at, :] = direction.astype(jnp.bfloat16)

        if step == 0:
            mine.start()
            spread(update.at[mp], mp)
        else:
            to_head(step).start()

    stores = [
        pltpu.make_async_copy(src, dst, store_sem.at[i])
        for i, (src, dst) in enumerate(
            ((w_out, new_master_ref), (m_out, new_first_ref), (v_out, new_second_ref))
        )
    ]
    for copy in stores:
        copy.start()

    for step in range(1, heads):
        head = lax.rem(mp + heads - step, heads)
        to_head(step).wait_recv()
        spread(block(head, dp), head)

    for far in range(1, line):
        for step in range(heads):
            head = lax.rem(mp + heads - step, heads)

            @pl.when(z - far >= 0)
            def _():
                at_z = z - far
                source = block(head, at_z * 2 + core)
                send_up(source, head, at_z).wait_recv()

                @pl.when(z < line - 1)
                def _():
                    send_up(source, head, at_z).start()

                send_mate(source, head, at_z).start()

            @pl.when(z + far < line)
            def _():
                at_z = z + far
                source = block(head, at_z * 2 + core)
                send_down(source, head, at_z).wait_recv()

                @pl.when(z > 0)
                def _():
                    send_down(source, head, at_z).start()

                send_mate(source, head, at_z).start()

    for at_z in range(line):
        for head in range(heads):
            source = block(head, at_z * 2 + core)
            send_mate(source, head, at_z).wait_recv()
            send_mate(source, head, at_z).wait_send()

            @pl.when((z < line - 1) & (z >= at_z))
            def _():
                send_up(source, head, at_z).wait_send()

            @pl.when((z > 0) & (z <= at_z))
            def _():
                send_down(source, head, at_z).wait_send()

    for step in range(1, heads):
        to_head(step).wait_send()
        norm_to_mp(step).wait_send()
    for step in range(1, dpn):
        norm_to_dp(step).wait_send()
    for dest in range(line):
        pair_act(dest).wait_send()

        @pl.when(z != dest)
        def _():
            @pl.loop(0, chunks)
            def _(chunk):
                for copy in hop(dest, 0, chunk):
                    copy.wait_send()

    for n in range(chunks):
        pair_vg(n).wait_send()
    mine.wait()
    for copy in stores:
        copy.wait()


def settle(*refs):
    count = (len(refs) - 1) // 2
    sem = refs[-1]
    copies = []
    for i in range(count):
        source, place = refs[i], refs[count + i]
        piece = source.shape[0] // PIECES[i]
        for j in range(PIECES[i]):
            at = pl.ds(j * piece, piece)
            copies.append(
                pltpu.make_async_copy(source.at[at], place.at[at], sem.at[len(copies)])
            )
    for copy in copies:
        copy.start()
    for copy in copies:
        copy.wait()


def one_kernel(line, heads, activations, value_grad, master, first_moment, second_moment, step_count):
    rows, cols = master.shape
    tokens = activations.shape[0]
    chunks = 4
    dpn = 2 * line
    clip_total = 0.5 * math.sqrt(rows * dpn * heads * cols)
    hbm = pl.BlockSpec(memory_space=pl.ANY)
    owned = jax.ShapeDtypeStruct((rows, cols), F32)
    wide = pltpu.VMEM((rows, cols), F32)
    dma = pltpu.SemaphoreType.DMA
    results = pl.pallas_call(
        functools.partial(kernel, line, heads, chunks, clip_total),
        out_shape=(
            owned,
            owned,
            owned,
            jax.ShapeDtypeStruct((rows * dpn * heads, cols // heads), jnp.bfloat16),
        ),
        in_specs=[pl.BlockSpec(memory_space=pltpu.SMEM)]
        + [hbm] * 5,
        out_specs=(hbm,) * 4,
        scratch_shapes=[
            pltpu.VMEM((line, 2 * tokens, rows), jnp.bfloat16),
            pltpu.VMEM((2 * tokens, cols), jnp.bfloat16),
            pltpu.VMEM((line, rows, cols), F32),
            pltpu.VMEM((line, chunks, rows, cols // chunks), jnp.int16),
            pltpu.VMEM((line, chunks, 1, cols // chunks), F32),
            pltpu.VMEM((2, line, chunks, rows, cols // chunks), jnp.int16),
            pltpu.VMEM((2, line, chunks, 1, cols // chunks), F32),
            pltpu.VMEM((dpn, 8, 128), F32),
            pltpu.VMEM((heads, 8, 128), F32),
            wide,
            wide,
            wide,
            wide,
            wide,
            wide,
            pltpu.VMEM((heads, rows, cols // heads), jnp.bfloat16),
            dma((line + chunks,)),
            dma((line + chunks,)),
            dma((line + chunks,)),
            dma((3,)),
            dma((2, line, chunks)),
            dma((2, 2, line, chunks)),
            dma((dpn,)),
            dma((dpn,)),
            dma((heads,)),
            dma((heads,)),
            dma((4,)),
            dma((heads,)),
            dma((heads,)),
            dma((line, heads)),
            dma((line, heads)),
            dma((line, heads)),
            dma((line, heads)),
            dma((line, heads)),
        ],
        compiler_params=pltpu.CompilerParams(
            collective_id=0, has_side_effects=True, vmem_limit_bytes=28 * 1024 * 1024
        ),
    )(
        step_count,
        *(
            pltpu.with_memory_space_constraint(x, pltpu.HBM)
            for x in (activations, value_grad, master, first_moment, second_moment)
        ),
    )
    shapes = tuple(jax.ShapeDtypeStruct(x.shape, x.dtype) for x in results)
    return pl.pallas_call(
        settle,
        out_shape=shapes,
        in_specs=[hbm] * 4,
        out_specs=(hbm,) * 4,
        scratch_shapes=[dma((sum(PIECES),))],
        compiler_params=pltpu.CompilerParams(vmem_limit_bytes=4 * 1024 * 1024),
    )(*(pltpu.with_memory_space_constraint(x, pltpu.VMEM) for x in results))


def plain(activations, value_grad, master, first_moment, second_moment, step_count):
    own_rows, cols = master.shape
    grad = lax.psum_scatter(
        lax.dot_general(
            activations, value_grad, (((0,), (0,)), ((), ())), preferred_element_type=F32
        ),
        "dp",
        scatter_dimension=0,
        tiled=True,
    )
    square_sum = lax.psum(jnp.sum(grad * grad), ("dp", "mp"))
    head_count = lax.axis_size("mp")
    clip_total = 0.5 * math.sqrt(own_rows * lax.axis_size("dp") * head_count * cols)
    factor = jnp.minimum(jnp.float32(1.0), clip_total / (jnp.sqrt(square_sum) + 1e-06))
    clipped = factor * grad
    new_first = 0.9 * first_moment + 0.1 * clipped
    new_second = 0.95 * second_moment + 0.05 * clipped * clipped
    scale_first, scale_second = adam_terms(step_count[0].astype(F32))
    direction = new_first * scale_first / (jnp.sqrt(new_second * scale_second) + 1e-08) + 0.1 * master
    new_master = master - 0.01 * direction
    update = direction.astype(jnp.bfloat16)
    received = lax.all_to_all(update, "mp", split_axis=1, concat_axis=0, tiled=True)
    stacked = received.reshape(head_count, own_rows, received.shape[1])
    gathered = lax.all_gather(stacked, "dp", axis=1, tiled=True)
    return (new_master, new_first, new_second, gathered.reshape(-1, gathered.shape[2]))


def solution(mesh):
    dpn, heads = mesh.shape["dp"], mesh.shape["mp"]

    def on_device(*args):
        rows, cols = args[2].shape
        if dpn % 4 == 0 and dpn <= 16 and rows % 128 == 0 and (cols // heads) % 128 == 0:
            return one_kernel(dpn // 2, heads, *args)
        return plain(*args)

    in_specs = (
        P("dp", "mp"),
        P("dp", None),
        P(("mp", "dp"), None),
        P(("mp", "dp"), None),
        P(("mp", "dp"), None),
        P(),
    )
    out_specs = (P(("mp", "dp"), None), P(("mp", "dp"), None), P(("mp", "dp"), None), P(None, "mp"))
    return jax.shard_map(
        on_device, mesh=mesh, in_specs=in_specs, out_specs=out_specs, check_vma=False
    )
```
